32 devices in a mesh: section: 4 (over x, core), row: 2 (over y), col: 4 (over z).
Axes of the slice: x: 2, y: 2, z: 4, core: 2. Of those that a mesh axis runs over, the one named last changes fastest.
Arguments:
- hidden: bfloat16 [4, 8, 4096], P(None, None, 'col'), may hold values from -6 to 6
- norm_gain: bfloat16 [4, 4096], P('section', 'col'), may hold values from 0.25 to 1.75
- w_qkv: bfloat16 [4, 4096, 6144], P('section', 'col', 'row'), may hold values from -0.09375 to 0.09375
- w_out: bfloat16 [4, 4096, 4096], P('section', 'row', 'col'), may hold values from -0.09375 to 0.09375
- cache_keys: bfloat16 [4, 4, 8, 128, 8, 128], P('section', None, 'col', None, 'row'), may hold values from -240 to 240, as said below
- cache_values: bfloat16 [4, 4, 8, 128, 8, 128], P('section', None, 'col', None, 'row'), may hold values from -6 to 6
- cache_lengths: int32 [4, 8], P(None, 'col'), may hold values from 1 to 127
Outputs:
- layer_outputs: bfloat16 [4, 4, 8, 4096], P('section', None, None, 'col')
The draws below stay inside these ranges and needn't reach their ends.
Inputs may be any that keep to these rules, and one draw needn't show every extreme that they name: `cache_keys`: cached keys are of order one except that some sequences may carry much larger keys at a few positions.
All inputs are finite; a program needn't handle non-finite values.
Results may differ from the reference program's by a relative error of at most 0.04.
Values may be sent and summed in bfloat16 or wider, within the bound.
No kernel may reach another device: no remote copies, remote signals or barrier semaphores. Data moves between devices by JAX's collectives and lax.ppermute only.
A program may use at most 64 MiB of HBM per device.

```python
import jax
import jax.numpy as jnp
from jax import lax

D = 4096
HEADS = 32
KVH = 8
HD = 128
MICRO = 4
LEN = 128
LAYERS = 4
BATCH = 8


def draw_cache_keys(key, part):
    normal_draw = jnp.clip(jax.random.normal(key, (LAYERS, MICRO, BATCH, LEN, KVH, HD), jnp.float32), -6.0, 6.0)
    return normal_draw.astype(jnp.bfloat16)


def touch_ends(drawn, rng, low, top_value):
    extent = drawn.shape
    spot = [jax.random.randint(jax.random.fold_in(rng, axis), (), 0, extent[axis]) for axis in range(len(extent))]
    drawn = drawn.at[tuple(spot)].set(low)
    longest = extent.index(max(extent))
    spot[longest] = (spot[longest] + 1) % extent[longest]
    return drawn.at[tuple(spot)].set(top_value)


def steps_of(rng, extent, pieces, smallest, top_value):
    loudness, own = 1.0, jax.random.fold_in(rng, 6)
    for position, blocks in pieces:
        draws = jnp.exp(jax.random.uniform(jax.random.fold_in(own, position), (blocks,), jnp.float32, smallest / len(pieces), top_value / len(pieces)))
        loudness = loudness * jnp.repeat(draws, extent[position] // blocks).reshape([-1 if axis == position else 1 for axis in range(len(extent))])
    return loudness


def noise(stream_key, extent, width, limit, cuts=(), kind=jnp.bfloat16):
    array = jax.random.normal(stream_key, extent, jnp.float32) * width
    if len(cuts) > 0:
        array = steps_of(stream_key, extent, cuts, -0.22, 0.18) * array
    return jnp.clip(array, min=-limit, max=limit).astype(kind)


def setup_inputs(seed: int = 0) -> dict:
    seeds = jax.random.split(jax.random.key(seed), 8)
    hidden = noise(seeds[0], (MICRO, BATCH, D), 1.0, 6.0, ((2, 4),))
    norm_gain = jnp.clip(1.0 + 0.15 * jax.random.normal(seeds[1], (LAYERS, D), jnp.float32), 0.25, 1.75).astype(jnp.bfloat16)
    w_qkv = noise(seeds[2], (LAYERS, D, (HEADS + 2 * KVH) * HD), D ** -0.5, 0.09375, ((0, 4), (1, 4), (2, 2)))
    w_out = noise(seeds[3], (LAYERS, HEADS * HD, D), (HEADS * HD) ** -0.5, 0.09375, ((0, 4), (1, 2), (2, 4)))
    cache_keys = draw_cache_keys(jax.random.fold_in(seeds[7], 71), 0)
    cache_values = noise(seeds[5], (LAYERS, MICRO, BATCH, LEN, KVH, HD), 1.0, 6.0, ((0, 4), (2, 4), (4, 2)))
    cache_lengths = touch_ends(jax.random.randint(seeds[6], (MICRO, BATCH), 1, LEN), jax.random.fold_in(seeds[6], 1), 1, LEN - 1).astype(jnp.int32)
    return {"hidden": hidden, "norm_gain": norm_gain, "w_qkv": w_qkv, "w_out": w_out, "cache_keys": cache_keys, "cache_values": cache_values, "cache_lengths": cache_lengths}


def rotate(vectors, positions):
    half_dim = vectors.shape[-1] // 2
    inverse_freq = 500000.0 ** (-jnp.arange(half_dim, dtype=jnp.float32) * 2.0 / vectors.shape[-1])
    angles = positions * inverse_freq
    angles = jnp.concatenate([angles, angles], axis=-1)
    swapped = jnp.concatenate([-vectors[..., half_dim:], vectors[..., :half_dim]], axis=-1)
    return vectors * jnp.cos(angles) + swapped * jnp.sin(angles)

def attend(queries, new_key, new_value, key_block, value_block, length):
    score_scale = 1.0 / jnp.sqrt(jnp.float32(queries.shape[-1]))
    scores = jnp.einsum('bgrd,bjgd->bgrj', queries.astype(jnp.float32), key_block.astype(jnp.float32)) * score_scale
    own_score = jnp.einsum('bgrd,bgd->bgr', queries.astype(jnp.float32), new_key.astype(jnp.float32)) * score_scale
    visible = jnp.arange(key_block.shape[1])[None, :] < length[:, None]
    scores = jnp.where(visible[:, None, None, :], scores, -jnp.inf)
    row_max = jnp.maximum(lax.optimization_barrier(jnp.max(scores, axis=-1)), own_score)
    cache_exp = jnp.exp(scores - row_max[..., None])
    own_exp = jnp.exp(own_score - row_max)
    total = lax.optimization_barrier(jnp.sum(cache_exp, axis=-1)) + own_exp
    cache_weight = (cache_exp / total[..., None]).astype(jnp.bfloat16)
    own_weight = (own_exp / total).astype(jnp.bfloat16)
    result = jnp.einsum('bgrj,bjgd->bgrd', cache_weight.astype(jnp.float32), value_block.astype(jnp.float32))
    result = result + own_weight.astype(jnp.float32)[..., None] * new_value.astype(jnp.float32)[:, :, None, :]
    return result.astype(jnp.bfloat16)

def heads_part(projected, key_block, value_block, length):
    per_group = projected.shape[2] - 2
    positions = length.astype(jnp.float32)
    queries = rotate(projected[:, :, :per_group], positions[:, None, None, None]).astype(jnp.bfloat16)
    new_key = rotate(projected[:, :, per_group], positions[:, None, None]).astype(jnp.bfloat16)
    new_value = projected[:, :, per_group + 1].astype(jnp.bfloat16)
    attended = attend(queries, new_key, new_value, key_block, value_block, length)
    return attended.reshape(attended.shape[0], -1)

def decoder_layer(current, gain_row, proj_weight, out_weight, key_block, value_block, length):
    h_float = current.astype(jnp.float32)
    scaled = (h_float * gain_row.astype(jnp.float32)).astype(jnp.bfloat16)
    squares = lax.optimization_barrier(jnp.sum(h_float * h_float, axis=1))
    factor = lax.rsqrt(squares / D + 1e-05)
    projected = jnp.dot(scaled, proj_weight, preferred_element_type=jnp.float32) * factor[:, None]
    projected = projected.reshape(current.shape[0], KVH, HEADS // KVH + 2, HD)
    attended = heads_part(projected, key_block, value_block, length)
    mixed_rows = jnp.dot(attended, out_weight, preferred_element_type=jnp.float32)
    return (h_float + mixed_rows).astype(jnp.bfloat16)

def reference(hidden, norm_gain, w_qkv, w_out, cache_keys, cache_values, cache_lengths):
    current = hidden
    collected = []
    for layer_at in range(LAYERS):
        produced = []
        for micro_at in range(MICRO):
            produced.append(decoder_layer(current[micro_at], norm_gain[layer_at], w_qkv[layer_at], w_out[layer_at], cache_keys[layer_at, micro_at], cache_values[layer_at, micro_at], cache_lengths[micro_at]))
        current = jnp.stack(produced)
        collected.append(current)
    return jnp.stack(collected)
```

```python
import jax
import jax.numpy as jnp
from jax import lax
from jax.sharding import PartitionSpec as P

D = 4096
HEADS = 32
KVH = 8


def rotation_tables(positions, head_dim):
    half_dim = head_dim // 2
    inverse_freq = 500000.0 ** (-jnp.arange(half_dim, dtype=jnp.float32) * 2.0 / head_dim)
    angles = positions[:, None] * inverse_freq
    cos, sin = jnp.cos(angles), jnp.sin(angles)
    return jnp.concatenate([cos, cos], axis=-1), jnp.concatenate([-sin, sin], axis=-1)


def rotate(vectors, cos, sin):
    half_dim = vectors.shape[-1] // 2
    swapped = jnp.concatenate([vectors[..., half_dim:], vectors[..., :half_dim]], axis=-1)
    return vectors * cos + swapped * sin


def attend(queries, new_key, new_value, keys, values, visible):
    score_scale = 1.0 / jnp.sqrt(jnp.float32(queries.shape[-1]))
    scores = (
        jnp.einsum("bgrd,bgjd->bgrj", queries, keys, preferred_element_type=jnp.float32)
        * score_scale
    )
    own_score = (
        jnp.sum(queries.astype(jnp.float32) * new_key.astype(jnp.float32)[:, :, None, :], axis=-1)
        * score_scale
    )
    scores = jnp.where(visible[:, None, None, :], scores, -jnp.inf)
    row_max = jnp.maximum(jnp.max(scores, axis=-1), own_score)
    cache_exp = jnp.exp(scores - row_max[..., None])
    own_exp = jnp.exp(own_score - row_max)
    total = jnp.sum(cache_exp, axis=-1) + own_exp
    cache_weight = (cache_exp / total[..., None]).astype(jnp.bfloat16)
    own_weight = (own_exp / total).astype(jnp.bfloat16)
    result = jnp.einsum("bgrj,bgjd->bgrd", cache_weight, values, preferred_element_type=jnp.float32)
    result = (
        result
        + own_weight.astype(jnp.float32)[..., None] * new_value.astype(jnp.float32)[:, :, None, :]
    )
    return result.astype(jnp.bfloat16)


def shards(hidden, norm_gain, w_qkv, w_out, cache_keys, cache_values, cache_lengths):
    sections = lax.axis_size("section")
    rows = lax.axis_size("row")
    cols = lax.axis_size("col")
    section_at = lax.axis_index("section")
    row_at = lax.axis_index("row")
    col_at = lax.axis_index("col")
    axes = ("section", "row", "col")
    micro, batch, width = hidden.shape
    seq_part = batch // cols
    chunk = micro * seq_part
    gain = norm_gain[0].astype(jnp.float32)
    groups, head_dim = cache_keys.shape[4:]
    per_group = HEADS // KVH
    length = cache_lengths.reshape(chunk)
    keys = cache_keys[0].transpose(0, 1, 3, 2, 4).reshape(chunk, groups, -1, head_dim)
    values = cache_values[0].transpose(0, 1, 3, 2, 4).reshape(chunk, groups, -1, head_dim)
    visible = jnp.arange(keys.shape[2])[None, :] < length[:, None]
    cos, sin = rotation_tables(length.astype(jnp.float32), head_dim)

    def flat(s, r, c):
        return (s * rows + r) * cols + c

    def send_col(x, section, by):
        pairs = [
            (flat(section, r, c), flat(section, r, (c + by) % cols))
            for r in range(rows)
            for c in range(cols)
        ]
        return lax.ppermute(x, axes, pairs)

    def send_row(x, froms, step, by):
        pairs = [
            (flat(s, r, c), flat(s + step, (r + by) % rows, c))
            for s in froms
            for r in range(rows)
            for c in range(cols)
        ]
        return lax.ppermute(x, axes, pairs)

    order = hidden.reshape(micro, cols, seq_part, width).transpose(1, 0, 2, 3)
    order = order.reshape(cols, chunk, width)
    order = jnp.concatenate([order, order], axis=0)
    current = lax.dynamic_slice_in_dim(order, col_at, cols, 0).reshape(cols * chunk, width)
    current = current.astype(jnp.float32)

    kept = None
    for tick in range(sections):
        scaled = (current * gain).astype(jnp.bfloat16)
        squares = jnp.sum(current * current, axis=1, keepdims=True)
        partial_value = jnp.dot(scaled, w_qkv[0], preferred_element_type=jnp.float32)
        high = lax.reduce_precision(squares, 8, 7)
        pad = jnp.zeros((cols * chunk, 126), jnp.float32)
        message = jnp.concatenate([partial_value, high, squares - high, pad], axis=1)
        message = message.astype(jnp.bfloat16)
        arrived = [
            send_col(message[k * chunk : (k + 1) * chunk], tick, k) for k in range(1, cols)
        ]
        projected = partial_value[:chunk]
        total_squares = squares[:chunk]
        features = projected.shape[1]
        for piece in arrived:
            wide = piece.astype(jnp.float32)
            projected = projected + wide[:, :features]
            total_squares = total_squares + (
                wide[:, features : features + 1] + wide[:, features + 1 : features + 2]
            )
        factor = lax.rsqrt(total_squares / D + 1e-05)
        projected = (projected * factor).reshape(chunk, groups, per_group + 2, head_dim)
        queries = rotate(
            projected[:, :, :per_group], cos[:, None, None], sin[:, None, None]
        ).astype(jnp.bfloat16)
        new_key = rotate(projected[:, :, per_group], cos[:, None], sin[:, None])
        new_key = new_key.astype(jnp.bfloat16)
        new_value = projected[:, :, per_group + 1].astype(jnp.bfloat16)
        attended = attend(queries, new_key, new_value, keys, values, visible)
        attended = attended.reshape(chunk, groups * per_group * head_dim)
        gathered = [attended] + [
            send_col(attended, tick, cols - k) for k in range(1, cols)
        ]
        mixed = jnp.dot(
            jnp.concatenate(gathered, axis=0), w_out[0], preferred_element_type=jnp.float32
        )
        own = (mixed + jnp.where(row_at == 0, current, 0.0)).astype(jnp.bfloat16)
        kept = own if kept is None else jnp.where(section_at == tick, own, kept)
        if tick + 1 < sections:
            parts = [send_row(own, [tick], 1, by) for by in range(rows)]
            if rows == 2:
                parts = [p.astype(jnp.float32) for p in parts]
                state = parts[0] + parts[1]
            else:
                parts = jnp.stack([p.astype(jnp.float32) for p in parts])
                parts = jnp.concatenate([parts, parts], axis=0)[::-1]
                state = jnp.sum(
                    lax.dynamic_slice_in_dim(parts, rows - 1 - row_at, rows, 0), axis=0
                )
            current = state.astype(jnp.bfloat16).astype(jnp.float32)

    everyone = list(range(sections))
    parts = [kept] + [send_row(kept, everyone, 0, by) for by in range(1, rows)]
    parts = [p.astype(jnp.float32) for p in parts]
    if rows == 2:
        state = parts[0] + parts[1]
    else:
        parts = jnp.stack(parts)
        parts = jnp.concatenate([parts, parts], axis=0)[::-1]
        state = jnp.sum(lax.dynamic_slice_in_dim(parts, rows - 1 - row_at, rows, 0), axis=0)
    state = state.astype(jnp.bfloat16).reshape(cols, chunk, width)
    state = jnp.concatenate([state, state], axis=0)
    state = lax.dynamic_slice_in_dim(state, (cols - col_at) % cols, cols, 0)
    state = state.reshape(cols, micro, seq_part, width).transpose(1, 0, 2, 3)
    return state.reshape(1, micro, batch, width)


def solution(mesh):
    return jax.shard_map(
        shards,
        mesh=mesh,
        in_specs=(
            P(None, None, "col"),
            P("section", "col"),
            P("section", "col", "row"),
            P("section", "row", "col"),
            P("section", None, "col", None, "row", None),
            P("section", None, "col", None, "row", None),
            P(None, "col"),
        ),
        out_specs=P("section", None, None, "col"),
        check_vma=False,
    )
```

```python
import jax
import jax.numpy as jnp
from jax import lax
from jax.sharding import PartitionSpec as P

D = 4096
HEADS = 32
KVH = 8


def rotation_tables(positions, head_dim):
    half_dim = head_dim // 2
    inverse_freq = 500000.0 ** (-jnp.arange(half_dim, dtype=jnp.float32) * 2.0 / head_dim)
    angles = positions[:, None] * inverse_freq
    cos, sin = jnp.cos(angles), jnp.sin(angles)
    return jnp.concatenate([cos, cos], axis=-1), jnp.concatenate([-sin, sin], axis=-1)


def rotate(vectors, cos, sin):
    half_dim = vectors.shape[-1] // 2
    swapped = jnp.concatenate([vectors[..., half_dim:], vectors[..., :half_dim]], axis=-1)
    return vectors * cos + swapped * sin


def attend(queries, new_key, new_value, keys, values, visible):
    score_scale = 1.0 / jnp.sqrt(jnp.float32(queries.shape[-1]))
    scores = (
        jnp.einsum("bgrd,bgjd->bgrj", queries, keys, preferred_element_type=jnp.float32)
        * score_scale
    )
    own_score = (
        jnp.sum(queries.astype(jnp.float32) * new_key.astype(jnp.float32)[:, :, None, :], axis=-1)
        * score_scale
    )
    scores = jnp.where(visible[:, None, None, :], scores, -jnp.inf)
    row_max = jnp.maximum(jnp.max(scores, axis=-1), own_score)
    cache_exp = jnp.exp(scores - row_max[..., None])
    own_exp = jnp.exp(own_score - row_max)
    total = jnp.sum(cache_exp, axis=-1) + own_exp
    cache_weight = (cache_exp / total[..., None]).astype(jnp.bfloat16)
    own_weight = (own_exp / total).astype(jnp.bfloat16)
    result = jnp.einsum("bgrj,bgjd->bgrd", cache_weight, values, preferred_element_type=jnp.float32)
    result = (
        result
        + own_weight.astype(jnp.float32)[..., None] * new_value.astype(jnp.float32)[:, :, None, :]
    )
    return result.astype(jnp.bfloat16)


def shards(hidden, norm_gain, w_qkv, w_out, cache_keys, cache_values, cache_lengths):
    sections = lax.axis_size("section")
    rows = lax.axis_size("row")
    cols = lax.axis_size("col")
    section_at = lax.axis_index("section")
    row_at = lax.axis_index("row")
    axes = ("section", "row", "col")
    micro, batch, width = hidden.shape
    seq_part = batch // cols
    chunk = micro * seq_part
    gain = norm_gain[0].astype(jnp.float32)
    groups, head_dim = cache_keys.shape[4:]
    per_group = HEADS // KVH
    length = cache_lengths.reshape(chunk)
    keys = cache_keys[0].transpose(0, 1, 3, 2, 4).reshape(chunk, groups, -1, head_dim)
    values = cache_values[0].transpose(0, 1, 3, 2, 4).reshape(chunk, groups, -1, head_dim)
    visible = jnp.arange(keys.shape[2])[None, :] < length[:, None]
    cos, sin = rotation_tables(length.astype(jnp.float32), head_dim)

    def flat(s, r, c):
        return (s * rows + r) * cols + c

    def spread(x):
        return lax.all_to_all(jnp.broadcast_to(x[None], (cols,) + x.shape), "col", 0, 0)

    def send_row(x, froms, step, by):
        pairs = [
            (flat(s, r, c), flat(s + step, (r + by) % rows, c))
            for s in froms
            for r in range(rows)
            for c in range(cols)
        ]
        return lax.ppermute(x, axes, pairs)

    current = hidden.reshape(micro, cols, seq_part, width).transpose(1, 0, 2, 3)
    current = current.reshape(cols * chunk, width)
    current = current.astype(jnp.float32)

    kept = None
    for tick in range(sections):
        scaled = (current * gain).astype(jnp.bfloat16)
        squares = jnp.sum(current * current, axis=1, keepdims=True)
        partial_value = jnp.dot(scaled, w_qkv[0], preferred_element_type=jnp.float32)
        high = lax.reduce_precision(squares, 8, 7)
        pad = jnp.zeros((cols * chunk, 126), jnp.float32)
        message = jnp.concatenate([partial_value, high, squares - high, pad], axis=1)
        message = message.astype(jnp.bfloat16)
        message = message.reshape(cols, chunk, message.shape[1])
        arrived = jnp.sum(lax.all_to_all(message, "col", 0, 0).astype(jnp.float32), axis=0)
        features = partial_value.shape[1]
        projected = arrived[:, :features]
        total_squares = arrived[:, features : features + 1] + arrived[:, features + 1 : features + 2]
        factor = lax.rsqrt(total_squares / D + 1e-05)
        projected = (projected * factor).reshape(chunk, groups, per_group + 2, head_dim)
        queries = rotate(
            projected[:, :, :per_group], cos[:, None, None], sin[:, None, None]
        ).astype(jnp.bfloat16)
        new_key = rotate(projected[:, :, per_group], cos[:, None], sin[:, None])
        new_key = new_key.astype(jnp.bfloat16)
        new_value = projected[:, :, per_group + 1].astype(jnp.bfloat16)
        attended = attend(queries, new_key, new_value, keys, values, visible)
        attended = attended.reshape(chunk, groups * per_group * head_dim)
        gathered = spread(attended).reshape(cols * chunk, attended.shape[1])
        mixed = jnp.dot(gathered, w_out[0], preferred_element_type=jnp.float32)
        own = (mixed + jnp.where(row_at == 0, current, 0.0)).astype(jnp.bfloat16)
        kept = own if kept is None else jnp.where(section_at == tick, own, kept)
        if tick + 1 < sections:
            parts = [send_row(own, [tick], 1, by) for by in range(rows)]
            if rows == 2:
                parts = [p.astype(jnp.float32) for p in parts]
                state = parts[0] + parts[1]
            else:
                parts = jnp.stack([p.astype(jnp.float32) for p in parts])
                parts = jnp.concatenate([parts, parts], axis=0)[::-1]
                state = jnp.sum(
                    lax.dynamic_slice_in_dim(parts, rows - 1 - row_at, rows, 0), axis=0
                )
            current = state.astype(jnp.bfloat16).astype(jnp.float32)

    everyone = list(range(sections))
    parts = [kept] + [send_row(kept, everyone, 0, by) for by in range(1, rows)]
    parts = [p.astype(jnp.float32) for p in parts]
    if rows == 2:
        state = parts[0] + parts[1]
    else:
        parts = jnp.stack(parts)
        parts = jnp.concatenate([parts, parts], axis=0)[::-1]
        state = jnp.sum(lax.dynamic_slice_in_dim(parts, rows - 1 - row_at, rows, 0), axis=0)
    state = state.astype(jnp.bfloat16).reshape(cols, micro, seq_part, width)
    return state.transpose(1, 0, 2, 3).reshape(1, micro, batch, width)


def solution(mesh):
    return jax.shard_map(
        shards,
        mesh=mesh,
        in_specs=(
            P(None, None, "col"),
            P("section", "col"),
            P("section", "col", "row"),
            P("section", "row", "col"),
            P("section", None, "col", None, "row", None),
            P("section", None, "col", None, "row", None),
            P(None, "col"),
        ),
        out_specs=P("section", None, None, "col"),
        check_vma=False,
    )
```

```python
import jax
import jax.numpy as jnp
from jax import lax
from jax.sharding import PartitionSpec as P

D = 4096
HEADS = 32
KVH = 8


def rotation_tables(positions, head_dim):
    half_dim = head_dim // 2
    inverse_freq = 500000.0 ** (-jnp.arange(half_dim, dtype=jnp.float32) * 2.0 / head_dim)
    angles = positions[:, None] * inverse_freq
    cos, sin = jnp.cos(angles), jnp.sin(angles)
    return jnp.concatenate([cos, cos], axis=-1), jnp.concatenate([-sin, sin], axis=-1)


def rotate(vectors, cos, sin):
    half_dim = vectors.shape[-1] // 2
    swapped = jnp.concatenate([vectors[..., half_dim:], vectors[..., :half_dim]], axis=-1)
    return vectors * cos + swapped * sin


def attend(queries, new_key, new_value, keys, values, visible):
    score_scale = 1.0 / jnp.sqrt(jnp.float32(queries.shape[-1]))
    scores = (
        jnp.einsum("bgrd,bgjd->bgrj", queries, keys, preferred_element_type=jnp.float32)
        * score_scale
    )
    own_score = (
        jnp.sum(queries.astype(jnp.float32) * new_key.astype(jnp.float32)[:, :, None, :], axis=-1)
        * score_scale
    )
    scores = jnp.where(visible[:, None, None, :], scores, -jnp.inf)
    row_max = jnp.maximum(jnp.max(scores, axis=-1), own_score)
    cache_exp = jnp.exp(scores - row_max[..., None])
    own_exp = jnp.exp(own_score - row_max)
    total = jnp.sum(cache_exp, axis=-1) + own_exp
    cache_weight = (cache_exp / total[..., None]).astype(jnp.bfloat16)
    own_weight = (own_exp / total).astype(jnp.bfloat16)
    result = jnp.einsum("bgrj,bgjd->bgrd", cache_weight, values, preferred_element_type=jnp.float32)
    result = (
        result
        + own_weight.astype(jnp.float32)[..., None] * new_value.astype(jnp.float32)[:, :, None, :]
    )
    return result.astype(jnp.bfloat16)


def shards(hidden, norm_gain, w_qkv, w_out, cache_keys, cache_values, cache_lengths):
    sections = lax.axis_size("section")
    rows = lax.axis_size("row")
    cols = lax.axis_size("col")
    section_at = lax.axis_index("section")
    row_at = lax.axis_index("row")
    axes = ("section", "row", "col")
    micro, batch, width = hidden.shape
    seq_part = batch // cols
    chunk = micro * seq_part
    gain = norm_gain[0].astype(jnp.float32)
    groups, head_dim = cache_keys.shape[4:]
    per_group = HEADS // KVH
    length = cache_lengths.reshape(chunk)
    keys = cache_keys[0].transpose(0, 1, 3, 2, 4).reshape(chunk, groups, -1, head_dim)
    values = cache_values[0].transpose(0, 1, 3, 2, 4).reshape(chunk, groups, -1, head_dim)
    visible = jnp.arange(keys.shape[2])[None, :] < length[:, None]
    cos, sin = rotation_tables(length.astype(jnp.float32), head_dim)

    def flat(s, r, c):
        return (s * rows + r) * cols + c

    def spread(x):
        return lax.all_to_all(jnp.broadcast_to(x[None], (cols,) + x.shape), "col", 0, 0)

    def send_row(x, froms, step, by):
        pairs = [
            (flat(s, r, c), flat(s + step, (r + by) % rows, c))
            for s in froms
            for r in range(rows)
            for c in range(cols)
        ]
        return lax.ppermute(x, axes, pairs)

    blocks = [hidden[m, c * seq_part : (c + 1) * seq_part] for c in range(cols) for m in range(micro)]
    current = jnp.concatenate([b.astype(jnp.float32) for b in blocks], axis=0)


    kept = None
    for tick in range(sections):
        scaled = (current * gain).astype(jnp.bfloat16)
        squares = jnp.sum(current * current, axis=1, keepdims=True)
        partial_value = jnp.dot(scaled, w_qkv[0], preferred_element_type=jnp.float32)
        high = lax.reduce_precision(squares, 8, 7)
        pad = jnp.zeros((cols * chunk, 126), jnp.float32)
        message = jnp.concatenate([partial_value, high, squares - high, pad], axis=1)
        message = message.astype(jnp.bfloat16)
        message = message.reshape(cols, chunk, message.shape[1])
        arrived = jnp.sum(lax.all_to_all(message, "col", 0, 0).astype(jnp.float32), axis=0)
        features = partial_value.shape[1]
        projected = arrived[:, :features]
        total_squares = arrived[:, features : features + 1] + arrived[:, features + 1 : features + 2]
        factor = lax.rsqrt(total_squares / D + 1e-05)
        projected = (projected * factor).reshape(chunk, groups, per_group + 2, head_dim)
        queries = rotate(
            projected[:, :, :per_group], cos[:, None, None], sin[:, None, None]
        ).astype(jnp.bfloat16)
        new_key = rotate(projected[:, :, per_group], cos[:, None], sin[:, None])
        new_key = new_key.astype(jnp.bfloat16)
        new_value = projected[:, :, per_group + 1].astype(jnp.bfloat16)
        attended = attend(queries, new_key, new_value, keys, values, visible)
        attended = attended.reshape(chunk, groups * per_group * head_dim)
        gathered = spread(attended).reshape(cols * chunk, attended.shape[1])
        mixed = jnp.dot(gathered, w_out[0], preferred_element_type=jnp.float32)
        own = (mixed + jnp.where(row_at == 0, current, 0.0)).astype(jnp.bfloat16)
        kept = own if kept is None else jnp.where(section_at == tick, own, kept)
        if tick + 1 < sections:
            parts = [send_row(own, [tick], 1, by) for by in range(rows)]
            if rows == 2:
                parts = [p.astype(jnp.float32) for p in parts]
                state = parts[0] + parts[1]
            else:
                parts = jnp.stack([p.astype(jnp.float32) for p in parts])
                parts = jnp.concatenate([parts, parts], axis=0)[::-1]
                state = jnp.sum(
                    lax.dynamic_slice_in_dim(parts, rows - 1 - row_at, rows, 0), axis=0
                )
            current = state.astype(jnp.bfloat16).astype(jnp.float32)

    everyone = list(range(sections))
    parts = [kept] + [send_row(kept, everyone, 0, by) for by in range(1, rows)]
    parts = [p.astype(jnp.float32) for p in parts]
    if rows == 2:
        state = parts[0] + parts[1]
    else:
        parts = jnp.stack(parts)
        parts = jnp.concatenate([parts, parts], axis=0)[::-1]
        state = jnp.sum(lax.dynamic_slice_in_dim(parts, rows - 1 - row_at, rows, 0), axis=0)
    state = state.astype(jnp.bfloat16).reshape(cols, micro, seq_part, width)
    return state.transpose(1, 0, 2, 3).reshape(1, micro, batch, width)


def solution(mesh):
    return jax.shard_map(
        shards,
        mesh=mesh,
        in_specs=(
            P(None, None, "col"),
            P("section", "col"),
            P("section", "col", "row"),
            P("section", "row", "col"),
            P("section", None, "col", None, "row", None),
            P("section", None, "col", None, "row", None),
            P(None, "col"),
        ),
        out_specs=P("section", None, None, "col"),
        check_vma=False,
    )
```
